32 devices in a mesh: scene: 8 (over z, y), image: 4 (over x, core).
Axes of the slice: x: 2, y: 2, z: 4, core: 2. Of those that a mesh axis runs over, the one named last changes fastest.
Arguments:
- jacobian: bfloat16 [256, 256, 1152], P(('scene', 'image')), may hold values from -0.1875 to 0.1875
- splat_ids: int32 [256, 128], P(('scene', 'image')), may hold values from 0 to 8191, as said below
- pix_residual: bfloat16 [256, 256], P(('scene', 'image')), may hold values from -6 to 6
- live_blocks: int32 [32], replicated, may hold values from 1 to 8, as said below
- proj_jac: bfloat16 [9, 59, 8192], P(None, None, 'scene'), may hold values from -0.75 to 0.75
- damping: float32 [59, 8192], P(None, 'scene'), may hold values from 0.1 to 1
- precond: float32 [59, 8192], P(None, 'scene'), may hold values from 0.3 to 9
Outputs:
- solution: float32 [59, 8192], P(None, 'scene')
- residual: float32 [59, 8192], P(None, 'scene')
The draws below stay inside these ranges and needn't reach their ends.
Inputs may be any that keep to these rules, and one draw needn't show every extreme that they name: live_blocks[d] counts the blocks in use on device d = scene index * 4 + image index; they are its slots 0 to live_blocks[d] - 1; some device uses all 8 while the device whose index differs from it in the lowest bit uses at most half of them. `splat_ids`: splat s of every block names a Gaussian of scene index s // 16, that is an id from that index times 1024 to the next such multiple.
All inputs are finite; a program needn't handle non-finite values.
Results may differ from the reference program's by a relative error of at most 0.0051.
Values may be sent and summed in bfloat16 or wider, within the bound.
A program may use at most 64 MiB of HBM per device.

```python
import math
import jax
import jax.numpy as jnp
from jax import lax

PAR = 59
PROJ = 9
PIX = 256
SPL = 128
ITERS = 2
G_DEV = 1024
BLK_DEV = 8
G = 8192
BLOCKS = 256
N_SCENE = 8
DEVICES = 32


def draw_live_blocks(key, part):
    first_key, second_key, third_key = jax.random.split(key, 3)
    lower_counts = jax.random.randint(first_key, (DEVICES,), 1, BLK_DEV // 2 + 1)
    heavy_mask = jax.random.randint(second_key, (DEVICES,), 0, 4) == 0
    counts = jnp.where(heavy_mask, BLK_DEV, lower_counts)
    chosen_device = jax.random.randint(third_key, (), 0, DEVICES)
    partner_device = jnp.bitwise_xor(chosen_device, 1)
    counts = counts.at[chosen_device].set(BLK_DEV)
    counts = counts.at[partner_device].set(lower_counts[partner_device])
    return counts.astype(jnp.int32)


def draw_splat_ids(key, part):
    owner_width = SPL // N_SCENE
    owners = jnp.arange(SPL, dtype=jnp.int32) // owner_width
    local_ids = jax.random.randint(key, (BLOCKS, SPL), 0, G_DEV)
    return (owners[None, :] * G_DEV + local_ids).astype(jnp.int32)


def draw_precond(key, part):
    ramp = 1.0 + 2.0 * jnp.arange(G, dtype=jnp.float32) / max(G - 1, 1)
    values = jnp.exp(jax.random.uniform(key, (PAR, G), jnp.float32, math.log(0.3), math.log(3.0)))
    return values * ramp[None, :]


def shard_levels(stream_key, extent, cuts, smallest, top_value):
    def one(dim, parts):
        draws = jax.random.uniform(jax.random.fold_in(jax.random.fold_in(stream_key, 6), dim), (parts,), jnp.float32, smallest / len(cuts), top_value / len(cuts))
        return jnp.repeat(jnp.exp(draws), extent[dim] // parts).reshape((-1,) + (1,) * (len(extent) - dim - 1))

    level = one(*cuts[0])
    for cut in cuts[1:]:
        level = level * one(*cut)
    return level


def centred(rng, extent, scale, bound, cuts=(), kind=jnp.bfloat16):
    values = scale * jax.random.normal(rng, extent, jnp.float32)
    if cuts:
        values = values * shard_levels(rng, extent, cuts, -0.22, 0.18)
    return jnp.clip(values, -bound, bound).astype(kind)


def setup_inputs(seed: int = 0) -> dict:
    splits = jax.random.split(jax.random.key(seed), 8)
    return {
        "jacobian": centred(splits[0], (BLOCKS, PIX, PROJ * SPL), (PROJ * SPL) ** -0.5, 0.1875, ((0, 32),)),
        "splat_ids": draw_splat_ids(jax.random.fold_in(splits[7], 71), 0),
        "pix_residual": centred(splits[2], (BLOCKS, PIX), 1.0, 6.0, ((0, 32),)),
        "live_blocks": draw_live_blocks(jax.random.fold_in(splits[7], 71), 0),
        "proj_jac": centred(splits[4], (PROJ, PAR, G), PAR ** -0.5, 0.75, ((2, 8),)),
        "damping": jnp.clip(jnp.exp(math.log(1.0) - 2.3025851 * jax.random.uniform(splits[5], (PAR, G), jnp.float32) ** shard_levels(splits[5], (PAR, G), ((1, 8),), -0.2, 0.2)), 0.1, 1.0),
        "precond": draw_precond(jax.random.fold_in(splits[7], 71), 0),
    }


def project(proj_jac, field):
    return jnp.einsum("kag,ag->kg", proj_jac.astype(jnp.float32), field, precision=lax.Precision.HIGHEST).astype(jnp.bfloat16)


def lift(proj_jac, weights):
    return jnp.einsum("kag,kg->ag", proj_jac.astype(jnp.float32), weights, precision=lax.Precision.HIGHEST)


def reference(jacobian, splat_ids, pix_residual, live_blocks, proj_jac, damping, precond):
    n_proj = proj_jac.shape[0]
    n_gauss = damping.shape[1]
    positions = jnp.arange(jacobian.shape[0], dtype=jnp.int32)
    active = (positions % BLK_DEV < live_blocks[positions // BLK_DEV]).astype(jnp.float32)

    def back_project(vectors):
        def advance(summed, pieces):
            jac_block, chosen, pixels, weight = pieces
            if vectors is None:
                signal = pixels
            else:
                picked = vectors[:, chosen].reshape(-1)
                signal = jnp.dot(jac_block, picked, preferred_element_type=jnp.float32).astype(jnp.bfloat16)
            returned = jnp.dot(signal, jac_block, preferred_element_type=jnp.float32) * weight
            return summed.at[:, chosen].add(returned.reshape(n_proj, -1)), None

        start = jnp.zeros((n_proj, n_gauss), jnp.float32)
        summed, _ = lax.scan(advance, start, (jacobian, splat_ids, pix_residual, active))
        return summed

    def operator(direction):
        return lift(proj_jac, back_project(project(proj_jac, direction))) + damping * direction

    residual = -lift(proj_jac, back_project(None))
    solution = jnp.zeros_like(residual)
    precon_res = precond * residual
    direction = precon_res
    rz_now = jnp.sum(residual * precon_res)
    for iteration in range(ITERS):
        image = operator(direction)
        alpha = rz_now / jnp.sum(direction * image)
        solution = solution + alpha * direction
        residual = residual - alpha * image
        precon_res = precond * residual
        rz_next = jnp.sum(residual * precon_res)
        direction = precon_res + (rz_next / rz_now) * direction
        rz_now = rz_next
    return solution, residual
```

```python
import functools

import jax
import jax.numpy as jnp
from jax import lax
from jax.experimental import pallas as pl
from jax.experimental.pallas import tpu as pltpu
from jax.sharding import PartitionSpec as P

ITERS = 2
LANES = 128
ROWS = 16
F32 = jnp.float32
BF16 = jnp.bfloat16
MESH = pl.DeviceIdType.MESH


def split3(x):
    hi = x.astype(BF16)
    rest = x - hi.astype(F32)
    mid = rest.astype(BF16)
    low = (rest - mid.astype(F32)).astype(BF16)
    return hi, mid, low


def swap_groups(x, n):
    w = LANES // n
    row = lax.broadcasted_iota(jnp.int32, x.shape, 0)
    lane = lax.broadcasted_iota(jnp.int32, x.shape, 1)
    m = 1
    while m < n:
        row_bit = (row & m) != 0
        lane_bit = (lane & (m * w)) != 0
        up = pltpu.roll(pltpu.roll(x, n - m, 0), w * m, 1)
        down = pltpu.roll(pltpu.roll(x, m, 0), LANES - w * m, 1)
        x = jnp.where(row_bit == lane_bit, x, jnp.where(lane_bit, up, down))
        m *= 2
    return x


def nt(a, b):
    return lax.dot_general(a, b, (((1,), (1,)), ((), ())), preferred_element_type=F32)


def kernel(
    n, n_img,
    live_ref, ids_ref, pix_ref, jac_hbm, proj_hbm, damp_hbm, prec_hbm,
    sol_ref, res_ref,
    jac, proj, damp, prec, hot, direc, ufield,
    id_send, id_recv, back_send, back_recv, gath_send, gath_recv, sum_own, sum_recv,
    load_sem, ssem, rsem, issem, irsem,
):
    n_blk, n_pix, width = jac.shape
    n_proj, n_par, g_dev = proj.shape
    me = lax.axis_index("scene")
    img = lax.axis_index("image")
    device_pos = me * n_img + img

    loads = [pltpu.make_async_copy(jac_hbm.at[b], jac.at[b], load_sem.at[b]) for b in range(n_blk)]
    loads.append(pltpu.make_async_copy(proj_hbm, proj, load_sem.at[n_blk]))
    loads.append(pltpu.make_async_copy(damp_hbm, damp, load_sem.at[n_blk + 1]))
    loads.append(pltpu.make_async_copy(prec_hbm, prec, load_sem.at[n_blk + 2]))
    for load in loads:
        load.start()

    scene_peers = [lax.rem(me + r, n) for r in range(1, n)]
    image_peers = [lax.rem(img + r, n_img) for r in range(1, n_img)]
    barrier = pltpu.get_barrier_semaphore()
    for peer in scene_peers:
        pl.semaphore_signal(barrier, inc=1, device_id={"scene": peer}, device_id_type=MESH)
    for peer in image_peers:
        pl.semaphore_signal(barrier, inc=1, device_id={"image": peer}, device_id_type=MESH)

    live = live_ref[device_pos]
    sends = []

    def exchange(phase, send, recv):
        copies = []
        for r, peer in enumerate(scene_peers):
            copy = pltpu.make_async_remote_copy(
                src_ref=send.at[peer], dst_ref=recv.at[me],
                send_sem=ssem.at[phase, r], recv_sem=rsem.at[phase, r],
                device_id={"scene": peer}, device_id_type=MESH,
            )
            copy.start()
            copies.append(copy)
        recv[me] = send[me]
        sends.extend(copies)
        return copies

    def image_exchange(phase):
        copies = []
        for r, peer in enumerate(image_peers):
            copy = pltpu.make_async_remote_copy(
                src_ref=sum_own.at[phase], dst_ref=sum_recv.at[phase, img],
                send_sem=issem.at[phase, r], recv_sem=irsem.at[phase, r],
                device_id={"image": peer}, device_id_type=MESH,
            )
            copy.start()
            copies.append(copy)
        sum_recv[phase, img] = sum_own[phase]
        sends.extend(copies)
        return copies

    def arrived(copies):
        for copy in copies:
            copy.wait_recv()

    def pad_rows(x, fill):
        if n == n_blk:
            return x
        return jnp.concatenate([x, jnp.full((n - n_blk, LANES), fill, x.dtype)], axis=0)

    block_row = lax.broadcasted_iota(jnp.int32, (n_blk, width), 0)
    pix_row = lax.broadcasted_iota(jnp.int32, (n_blk, n_pix), 0)
    msg_row = lax.broadcasted_iota(jnp.int32, (ROWS, LANES), 0)

    def returned(signals, first):
        total = jnp.zeros((n_blk, width), F32)
        for b in range(n_blk):
            if first:
                loads[b].wait()
            one = jnp.dot(signals, jac[b], preferred_element_type=F32)
            total = jnp.where(block_row == b, one, total)
        return jnp.where(block_row < live, total, 0.0)

    def block_images(vectors):
        total = jnp.zeros((n_blk, n_pix), F32)
        for b in range(n_blk):
            total = jnp.where(pix_row == b, nt(vectors, jac[b]), total)
        return total.astype(BF16)

    def lane_sums(x):
        rows = jnp.sum(x, axis=0, keepdims=True)
        total = rows[:, :LANES]
        for c in range(1, x.shape[1] // LANES):
            total = total + rows[:, c * LANES:(c + 1) * LANES]
        return total

    def send_back(phase, back, extras):
        send, recv = back_send.at[phase], back_recv.at[phase]
        for k in range(n_proj):
            piece = pad_rows(back[:, k * LANES:(k + 1) * LANES], 0.0)
            send[:, k, :] = swap_groups(piece, n)
        for k in range(n_proj, ROWS):
            extra = extras[k - n_proj] if k - n_proj < len(extras) else jnp.zeros((1, LANES), F32)
            send[:, k, :] = jnp.broadcast_to(extra, (n, LANES))
        return exchange(1 + 2 * phase, send, recv)

    def reduce_back(phase, copies):
        arrived(copies)
        recv = back_recv.at[phase]
        arrivals = jnp.concatenate([recv[j] for j in range(n)], axis=1)
        parts = jnp.concatenate(split3(arrivals), axis=0)
        summed = nt(parts, hot[...])
        summed = summed[:ROWS] + summed[ROWS:2 * ROWS] + summed[2 * ROWS:]
        extras = recv[0]
        for j in range(1, n):
            extras = extras + recv[j]
        tail = g_dev + LANES
        sum_own[phase, :, :g_dev] = summed[:8]
        for c in range(g_dev // LANES):
            sum_own[phase, c:c + 1, g_dev:tail] = summed[8:9, c * LANES:(c + 1) * LANES]
        sum_own[phase, :, tail:] = jnp.where(
            msg_row[:8] == 0, extras[n_proj:n_proj + 1], 0.0
        )
        arrived(image_exchange(phase))
        total = sum_recv[phase, 0]
        for i in range(1, n_img):
            total = total + sum_recv[phase, i]
        dot = jnp.sum(total[:, tail:], keepdims=True)
        side = jnp.sum(extras[n_proj + 1:n_proj + 2], keepdims=True)
        return total, dot, side

    def lifted(weights, cols):
        chunk = cols.start // LANES
        total = proj[8, :, cols].astype(F32) * weights[chunk:chunk + 1, g_dev:g_dev + LANES]
        for k in range(8):
            total = total + proj[k, :, cols].astype(F32) * weights[k:k + 1, cols]
        return total

    def chunks():
        return [slice(c * LANES, (c + 1) * LANES) for c in range(g_dev // LANES)]

    def project_chunk(field, cols):
        for k in range(n_proj):
            ufield[k:k + 1, cols] = jnp.sum(
                proj[k, :, cols].astype(F32) * field, axis=0, keepdims=True
            )

    def send_gathered(phase, extras):
        parts = jnp.concatenate(split3(ufield[...]), axis=0)
        picked = jnp.dot(parts, hot[...], preferred_element_type=F32)
        picked = picked[:ROWS] + picked[ROWS:2 * ROWS] + picked[2 * ROWS:]
        send, recv = gath_send.at[phase], gath_recv.at[phase]
        for j in range(n):
            piece = picked[:, j * LANES:(j + 1) * LANES]
            for k, extra in enumerate(extras):
                piece = jnp.where(msg_row == n_proj + k, extra, piece)
            send[j] = piece
        return exchange(2 + 2 * phase, send, recv)

    def take_gathered(phase, copies):
        arrived(copies)
        recv = gath_recv.at[phase]
        pieces = [swap_groups(recv[:, k, :], n)[:n_blk] for k in range(n_proj)]
        extras = recv[0]
        for j in range(1, n):
            extras = extras + recv[j]
        sums = jnp.sum(extras, axis=1, keepdims=True)
        return jnp.concatenate(pieces, axis=1), sums[n_proj:n_proj + 1], sums[n_proj + 1:n_proj + 2]

    routed = swap_groups(pad_rows(ids_ref[...], -1), n)
    id_send[:, 0, :] = routed
    pl.semaphore_wait(barrier, n - 1 + n_img - 1)
    id_copies = exchange(0, id_send, id_recv)

    back = returned(pix_ref[...], True)
    copies = send_back(0, back, [])

    arrived(id_copies)
    ufield[...] = jnp.zeros_like(ufield)
    g_iota = lax.broadcasted_iota(jnp.int32, (g_dev, LANES), 0)
    for j in range(n):
        local_ids = id_recv[j] - me * g_dev
        hot[:, j * LANES:(j + 1) * LANES] = jnp.where(g_iota == local_ids, 1.0, 0.0).astype(BF16)
    for load in loads[n_blk:]:
        load.wait()

    weights, _, _ = reduce_back(0, copies)
    rz_part = jnp.zeros((1, LANES), F32)
    dd_part = jnp.zeros((1, LANES), F32)
    for cols in chunks():
        residual = -lifted(weights, cols)
        res_ref[:, cols] = residual
        z = prec[:, cols] * residual
        direc[:, cols] = z
        rz_part = rz_part + jnp.sum(residual * z, axis=0, keepdims=True)
        dd_part = dd_part + jnp.sum(damp[:, cols] * z * z, axis=0, keepdims=True)
        project_chunk(z, cols)
    copies = send_gathered(0, [rz_part, dd_part])

    vectors = rz_now = None
    for iteration in range(ITERS):
        if iteration == 0:
            vectors, rz_now, dd = take_gathered(0, copies)
            extras = []
        else:
            gathered, rz_next, _ = take_gathered(iteration, copies)
            beta = rz_next / rz_now
            rz_now = rz_next
            vectors = gathered + beta * vectors
            dd_part = jnp.zeros((1, LANES), F32)
            for cols in chunks():
                d = prec[:, cols] * res_ref[:, cols] + beta * direc[:, cols]
                direc[:, cols] = d
                dd_part = dd_part + jnp.sum(damp[:, cols] * d * d, axis=0, keepdims=True)
            extras = [dd_part]
        back = returned(block_images(vectors.astype(BF16)), False)
        copies = send_back(iteration + 1, back, [lane_sums(back * vectors)] + extras)
        weights, dot, side = reduce_back(iteration + 1, copies)
        alpha = rz_now / (dot + (dd if iteration == 0 else side))
        last = iteration == ITERS - 1
        rz_part = jnp.zeros((1, LANES), F32)
        for cols in chunks():
            d = direc[:, cols]
            image = lifted(weights, cols) + damp[:, cols] * d
            residual = res_ref[:, cols] - alpha * image
            res_ref[:, cols] = residual
            sol_ref[:, cols] = alpha * d if iteration == 0 else sol_ref[:, cols] + alpha * d
            if not last:
                z = prec[:, cols] * residual
                rz_part = rz_part + jnp.sum(residual * z, axis=0, keepdims=True)
                project_chunk(z, cols)
        if not last:
            copies = send_gathered(iteration + 1, [rz_part])
    for copy in sends:
        copy.wait_send()


def local(n, n_img, jacobian, splat_ids, pix_residual, live_blocks, proj_jac, damping, precond):
    n_blk, n_pix, width = jacobian.shape
    n_proj, n_par, g_dev = proj_jac.shape
    field = (n_par, g_dev)
    phases = 2 * ITERS + 2
    vmem = pl.BlockSpec(memory_space=pltpu.VMEM)
    hbm = pl.BlockSpec(memory_space=pl.ANY)
    return pl.pallas_call(
        functools.partial(kernel, n, n_img),
        out_shape=[jax.ShapeDtypeStruct(field, F32)] * 2,
        in_specs=[pl.BlockSpec(memory_space=pltpu.SMEM), vmem, vmem, hbm, hbm, hbm, hbm],
        out_specs=[vmem, vmem],
        scratch_shapes=[
            pltpu.VMEM(jacobian.shape, BF16),
            pltpu.VMEM(proj_jac.shape, BF16),
            pltpu.VMEM(field, F32),
            pltpu.VMEM(field, F32),
            pltpu.VMEM((g_dev, n * LANES), BF16),
            pltpu.VMEM(field, F32),
            pltpu.VMEM((ROWS, g_dev), F32),
            pltpu.VMEM((n, 1, LANES), jnp.int32),
            pltpu.VMEM((n, 1, LANES), jnp.int32),
            pltpu.VMEM((ITERS + 1, n, ROWS, LANES), F32),
            pltpu.VMEM((ITERS + 1, n, ROWS, LANES), F32),
            pltpu.VMEM((ITERS, n, ROWS, LANES), F32),
            pltpu.VMEM((ITERS, n, ROWS, LANES), F32),
            pltpu.VMEM((ITERS + 1, 8, g_dev + 2 * LANES), F32),
            pltpu.VMEM((ITERS + 1, n_img, 8, g_dev + 2 * LANES), F32),
            pltpu.SemaphoreType.DMA((n_blk + 3,)),
            pltpu.SemaphoreType.DMA((phases, n - 1)),
            pltpu.SemaphoreType.DMA((phases, n - 1)),
            pltpu.SemaphoreType.DMA((ITERS + 1, n_img - 1)),
            pltpu.SemaphoreType.DMA((ITERS + 1, n_img - 1)),
        ],
        compiler_params=pltpu.CompilerParams(
            collective_id=0, has_side_effects=True, vmem_limit_bytes=50 * 1024 * 1024
        ),
    )(live_blocks, splat_ids, pix_residual, jacobian, proj_jac, damping, precond)


def solution(mesh):
    return jax.shard_map(
        functools.partial(local, mesh.shape["scene"], mesh.shape["image"]),
        mesh=mesh,
        in_specs=(
            P(("scene", "image"), None, None),
            P(("scene", "image"), None),
            P(("scene", "image"), None),
            P(),
            P(None, None, "scene"),
            P(None, "scene"),
            P(None, "scene"),
        ),
        out_specs=(P(None, "scene"), P(None, "scene")),
        check_vma=False,
    )
```

```python
import functools

import jax
import jax.numpy as jnp
from jax import lax
from jax.experimental import pallas as pl
from jax.experimental.pallas import tpu as pltpu
from jax.sharding import PartitionSpec as P

ITERS = 2
LANES = 128
ROWS = 16
F32 = jnp.float32
BF16 = jnp.bfloat16
MESH = pl.DeviceIdType.MESH


def split3(x):
    hi = x.astype(BF16)
    rest = x - hi.astype(F32)
    mid = rest.astype(BF16)
    low = (rest - mid.astype(F32)).astype(BF16)
    return hi, mid, low


def swap_groups(x, n):
    w = LANES // n
    row = lax.broadcasted_iota(jnp.int32, x.shape, 0)
    lane = lax.broadcasted_iota(jnp.int32, x.shape, 1)
    m = 1
    while m < n:
        row_bit = (row & m) != 0
        lane_bit = (lane & (m * w)) != 0
        up = pltpu.roll(pltpu.roll(x, n - m, 0), w * m, 1)
        down = pltpu.roll(pltpu.roll(x, m, 0), LANES - w * m, 1)
        x = jnp.where(row_bit == lane_bit, x, jnp.where(lane_bit, up, down))
        m *= 2
    return x


def nt(a, b):
    return lax.dot_general(a, b, (((1,), (1,)), ((), ())), preferred_element_type=F32)


def kernel(
    n, n_img,
    live_hbm, ids_hbm, pix_hbm, jac_hbm, proj_hbm, damp_hbm, prec_hbm,
    sol_ref, res_ref,
    live_ref, ids_ref, pix_ref, jac, proj, damp, prec, hot, direc, ufield,
    id_send, id_recv, back_send, back_recv, gath_send, gath_recv, sum_own, sum_recv,
    load_sem, ssem, rsem, issem, irsem,
):
    n_blk, n_pix, width = jac.shape
    n_proj, n_par, g_dev = proj.shape
    me = lax.axis_index("scene")
    img = lax.axis_index("image")
    device_pos = me * n_img + img

    small = [
        pltpu.make_async_copy(src, dst, load_sem.at[n_blk + 3 + i])
        for i, (src, dst) in enumerate(
            [(ids_hbm, ids_ref), (pix_hbm, pix_ref), (live_hbm, live_ref)]
        )
    ]
    for load in small:
        load.start()
    loads = [pltpu.make_async_copy(jac_hbm.at[b], jac.at[b], load_sem.at[b]) for b in range(n_blk)]
    loads.append(pltpu.make_async_copy(proj_hbm, proj, load_sem.at[n_blk]))
    loads.append(pltpu.make_async_copy(damp_hbm, damp, load_sem.at[n_blk + 1]))
    loads.append(pltpu.make_async_copy(prec_hbm, prec, load_sem.at[n_blk + 2]))
    for load in loads:
        load.start()

    scene_peers = [lax.rem(me + r, n) for r in range(1, n)]
    image_peers = [lax.rem(img + r, n_img) for r in range(1, n_img)]
    barrier = pltpu.get_barrier_semaphore()
    for peer in scene_peers:
        pl.semaphore_signal(barrier, inc=1, device_id={"scene": peer}, device_id_type=MESH)
    for peer in image_peers:
        pl.semaphore_signal(barrier, inc=1, device_id={"image": peer}, device_id_type=MESH)

    for load in small:
        load.wait()
    live = live_ref[device_pos]
    sends = []

    def exchange(phase, send, recv):
        copies = []
        for r, peer in enumerate(scene_peers):
            copy = pltpu.make_async_remote_copy(
                src_ref=send.at[peer], dst_ref=recv.at[me],
                send_sem=ssem.at[phase, r], recv_sem=rsem.at[phase, r],
                device_id={"scene": peer}, device_id_type=MESH,
            )
            copy.start()
            copies.append(copy)
        recv[me] = send[me]
        sends.extend(copies)
        return copies

    def image_exchange(phase):
        copies = []
        for r, peer in enumerate(image_peers):
            copy = pltpu.make_async_remote_copy(
                src_ref=sum_own.at[phase], dst_ref=sum_recv.at[phase, img],
                send_sem=issem.at[phase, r], recv_sem=irsem.at[phase, r],
                device_id={"image": peer}, device_id_type=MESH,
            )
            copy.start()
            copies.append(copy)
        sum_recv[phase, img] = sum_own[phase]
        sends.extend(copies)
        return copies

    def arrived(copies):
        for copy in copies:
            copy.wait_recv()

    def pad_rows(x, fill):
        if n == n_blk:
            return x
        return jnp.concatenate([x, jnp.full((n - n_blk, LANES), fill, x.dtype)], axis=0)

    block_row = lax.broadcasted_iota(jnp.int32, (n_blk, width), 0)
    pix_row = lax.broadcasted_iota(jnp.int32, (n_blk, n_pix), 0)
    msg_row = lax.broadcasted_iota(jnp.int32, (ROWS, LANES), 0)

    def returned(signals, first):
        total = jnp.zeros((n_blk, width), F32)
        for b in range(n_blk):
            if first:
                loads[b].wait()
            one = jnp.dot(signals, jac[b], preferred_element_type=F32)
            total = jnp.where(block_row == b, one, total)
        return jnp.where(block_row < live, total, 0.0)

    def block_images(vectors):
        total = jnp.zeros((n_blk, n_pix), F32)
        for b in range(n_blk):
            total = jnp.where(pix_row == b, nt(vectors, jac[b]), total)
        return total.astype(BF16)

    def lane_sums(x):
        rows = jnp.sum(x, axis=0, keepdims=True)
        total = rows[:, :LANES]
        for c in range(1, x.shape[1] // LANES):
            total = total + rows[:, c * LANES:(c + 1) * LANES]
        return total

    def send_back(phase, back, extras):
        send, recv = back_send.at[phase], back_recv.at[phase]
        for k in range(n_proj):
            piece = pad_rows(back[:, k * LANES:(k + 1) * LANES], 0.0)
            send[:, k, :] = swap_groups(piece, n)
        for k in range(n_proj, ROWS):
            extra = extras[k - n_proj] if k - n_proj < len(extras) else jnp.zeros((1, LANES), F32)
            send[:, k, :] = jnp.broadcast_to(extra, (n, LANES))
        return exchange(1 + 2 * phase, send, recv)

    def reduce_back(phase, copies):
        arrived(copies)
        recv = back_recv.at[phase]
        arrivals = jnp.concatenate([recv[j] for j in range(n)], axis=1)
        parts = jnp.concatenate(split3(arrivals), axis=0)
        summed = nt(parts, hot[...])
        summed = summed[:ROWS] + summed[ROWS:2 * ROWS] + summed[2 * ROWS:]
        extras = recv[0]
        for j in range(1, n):
            extras = extras + recv[j]
        tail = g_dev + LANES
        sum_own[phase, :, :g_dev] = summed[:8]
        for c in range(g_dev // LANES):
            sum_own[phase, c:c + 1, g_dev:tail] = summed[8:9, c * LANES:(c + 1) * LANES]
        sum_own[phase, :, tail:] = jnp.where(
            msg_row[:8] == 0, extras[n_proj:n_proj + 1], 0.0
        )
        arrived(image_exchange(phase))
        total = sum_recv[phase, 0]
        for i in range(1, n_img):
            total = total + sum_recv[phase, i]
        dot = jnp.sum(total[:, tail:], keepdims=True)
        side = jnp.sum(extras[n_proj + 1:n_proj + 2], keepdims=True)
        return total, dot, side

    def lifted(weights, cols):
        chunk = cols.start // LANES
        total = proj[8, :, cols].astype(F32) * weights[chunk:chunk + 1, g_dev:g_dev + LANES]
        for k in range(8):
            total = total + proj[k, :, cols].astype(F32) * weights[k:k + 1, cols]
        return total

    def chunks():
        return [slice(c * LANES, (c + 1) * LANES) for c in range(g_dev // LANES)]

    def project_chunk(field, cols):
        for k in range(n_proj):
            ufield[k:k + 1, cols] = jnp.sum(
                proj[k, :, cols].astype(F32) * field, axis=0, keepdims=True
            )

    def send_gathered(phase, extras):
        parts = jnp.concatenate(split3(ufield[...]), axis=0)
        picked = jnp.dot(parts, hot[...], preferred_element_type=F32)
        picked = picked[:ROWS] + picked[ROWS:2 * ROWS] + picked[2 * ROWS:]
        send, recv = gath_send.at[phase], gath_recv.at[phase]
        for j in range(n):
            piece = picked[:, j * LANES:(j + 1) * LANES]
            for k, extra in enumerate(extras):
                piece = jnp.where(msg_row == n_proj + k, extra, piece)
            send[j] = piece
        return exchange(2 + 2 * phase, send, recv)

    def take_gathered(phase, copies):
        arrived(copies)
        recv = gath_recv.at[phase]
        pieces = [swap_groups(recv[:, k, :], n)[:n_blk] for k in range(n_proj)]
        extras = recv[0]
        for j in range(1, n):
            extras = extras + recv[j]
        sums = jnp.sum(extras, axis=1, keepdims=True)
        return jnp.concatenate(pieces, axis=1), sums[n_proj:n_proj + 1], sums[n_proj + 1:n_proj + 2]

    routed = swap_groups(pad_rows(ids_ref[...], -1), n)
    id_send[:, 0, :] = routed
    pl.semaphore_wait(barrier, n - 1 + n_img - 1)
    id_copies = exchange(0, id_send, id_recv)

    back = returned(pix_ref[...], True)
    copies = send_back(0, back, [])

    arrived(id_copies)
    ufield[...] = jnp.zeros_like(ufield)
    g_iota = lax.broadcasted_iota(jnp.int32, (g_dev, LANES), 0)
    for j in range(n):
        local_ids = id_recv[j] - me * g_dev
        hot[:, j * LANES:(j + 1) * LANES] = jnp.where(g_iota == local_ids, 1.0, 0.0).astype(BF16)
    for load in loads[n_blk:]:
        load.wait()

    weights, _, _ = reduce_back(0, copies)
    rz_part = jnp.zeros((1, LANES), F32)
    dd_part = jnp.zeros((1, LANES), F32)
    for cols in chunks():
        residual = -lifted(weights, cols)
        res_ref[:, cols] = residual
        z = prec[:, cols] * residual
        direc[:, cols] = z
        rz_part = rz_part + jnp.sum(residual * z, axis=0, keepdims=True)
        dd_part = dd_part + jnp.sum(damp[:, cols] * z * z, axis=0, keepdims=True)
        project_chunk(z, cols)
    copies = send_gathered(0, [rz_part, dd_part])

    vectors = rz_now = None
    for iteration in range(ITERS):
        if iteration == 0:
            vectors, rz_now, dd = take_gathered(0, copies)
            extras = []
        else:
            gathered, rz_next, _ = take_gathered(iteration, copies)
            beta = rz_next / rz_now
            rz_now = rz_next
            vectors = gathered + beta * vectors
            dd_part = jnp.zeros((1, LANES), F32)
            for cols in chunks():
                d = prec[:, cols] * res_ref[:, cols] + beta * direc[:, cols]
                direc[:, cols] = d
                dd_part = dd_part + jnp.sum(damp[:, cols] * d * d, axis=0, keepdims=True)
            extras = [dd_part]
        back = returned(block_images(vectors.astype(BF16)), False)
        copies = send_back(iteration + 1, back, [lane_sums(back * vectors)] + extras)
        weights, dot, side = reduce_back(iteration + 1, copies)
        alpha = rz_now / (dot + (dd if iteration == 0 else side))
        last = iteration == ITERS - 1
        rz_part = jnp.zeros((1, LANES), F32)
        for cols in chunks():
            d = direc[:, cols]
            image = lifted(weights, cols) + damp[:, cols] * d
            residual = res_ref[:, cols] - alpha * image
            res_ref[:, cols] = residual
            sol_ref[:, cols] = alpha * d if iteration == 0 else sol_ref[:, cols] + alpha * d
            if not last:
                z = prec[:, cols] * residual
                rz_part = rz_part + jnp.sum(residual * z, axis=0, keepdims=True)
                project_chunk(z, cols)
        if not last:
            copies = send_gathered(iteration + 1, [rz_part])
    for copy in sends:
        copy.wait_send()


def local(n, n_img, jacobian, splat_ids, pix_residual, live_blocks, proj_jac, damping, precond):
    n_blk, n_pix, width = jacobian.shape
    n_proj, n_par, g_dev = proj_jac.shape
    field = (n_par, g_dev)
    phases = 2 * ITERS + 2
    vmem = pl.BlockSpec(memory_space=pltpu.VMEM)
    hbm = pl.BlockSpec(memory_space=pl.ANY)
    return pl.pallas_call(
        functools.partial(kernel, n, n_img),
        out_shape=[jax.ShapeDtypeStruct(field, F32)] * 2,
        in_specs=[hbm] * 7,
        out_specs=[vmem, vmem],
        scratch_shapes=[
            pltpu.SMEM(live_blocks.shape, jnp.int32),
            pltpu.VMEM(splat_ids.shape, jnp.int32),
            pltpu.VMEM(pix_residual.shape, BF16),
            pltpu.VMEM(jacobian.shape, BF16),
            pltpu.VMEM(proj_jac.shape, BF16),
            pltpu.VMEM(field, F32),
            pltpu.VMEM(field, F32),
            pltpu.VMEM((g_dev, n * LANES), BF16),
            pltpu.VMEM(field, F32),
            pltpu.VMEM((ROWS, g_dev), F32),
            pltpu.VMEM((n, 1, LANES), jnp.int32),
            pltpu.VMEM((n, 1, LANES), jnp.int32),
            pltpu.VMEM((ITERS + 1, n, ROWS, LANES), F32),
            pltpu.VMEM((ITERS + 1, n, ROWS, LANES), F32),
            pltpu.VMEM((ITERS, n, ROWS, LANES), F32),
            pltpu.VMEM((ITERS, n, ROWS, LANES), F32),
            pltpu.VMEM((ITERS + 1, 8, g_dev + 2 * LANES), F32),
            pltpu.VMEM((ITERS + 1, n_img, 8, g_dev + 2 * LANES), F32),
            pltpu.SemaphoreType.DMA((n_blk + 6,)),
            pltpu.SemaphoreType.DMA((phases, n - 1)),
            pltpu.SemaphoreType.DMA((phases, n - 1)),
            pltpu.SemaphoreType.DMA((ITERS + 1, n_img - 1)),
            pltpu.SemaphoreType.DMA((ITERS + 1, n_img - 1)),
        ],
        compiler_params=pltpu.CompilerParams(
            collective_id=0, has_side_effects=True, vmem_limit_bytes=67043328
        ),
    )(live_blocks, splat_ids, pix_residual, jacobian, proj_jac, damping, precond)


def solution(mesh):
    return jax.shard_map(
        functools.partial(local, mesh.shape["scene"], mesh.shape["image"]),
        mesh=mesh,
        in_specs=(
            P(("scene", "image"), None, None),
            P(("scene", "image"), None),
            P(("scene", "image"), None),
            P(),
            P(None, None, "scene"),
            P(None, "scene"),
            P(None, "scene"),
        ),
        out_specs=(P(None, "scene"), P(None, "scene")),
        check_vma=False,
    )
```

```python
import functools

import jax
import jax.numpy as jnp
from jax import lax
from jax.experimental import pallas as pl
from jax.experimental.pallas import tpu as pltpu
from jax.sharding import PartitionSpec as P

ITERS = 2
LANES = 128
ROWS = 16
F32 = jnp.float32
BF16 = jnp.bfloat16
MESH = pl.DeviceIdType.MESH


def split3(x):
    hi = x.astype(BF16)
    rest = x - hi.astype(F32)
    mid = rest.astype(BF16)
    low = (rest - mid.astype(F32)).astype(BF16)
    return hi, mid, low


def swap_groups(x, n):
    w = LANES // n
    row = lax.broadcasted_iota(jnp.int32, x.shape, 0)
    lane = lax.broadcasted_iota(jnp.int32, x.shape, 1)
    m = 1
    while m < n:
        row_bit = (row & m) != 0
        lane_bit = (lane & (m * w)) != 0
        up = pltpu.roll(pltpu.roll(x, n - m, 0), w * m, 1)
        down = pltpu.roll(pltpu.roll(x, m, 0), LANES - w * m, 1)
        x = jnp.where(row_bit == lane_bit, x, jnp.where(lane_bit, up, down))
        m *= 2
    return x


def nt(a, b):
    return lax.dot_general(a, b, (((1,), (1,)), ((), ())), preferred_element_type=F32)


def kernel(
    n, n_img,
    live_hbm, ids_hbm, pix_hbm, jac_hbm, proj_hbm, damp_hbm, prec_hbm,
    sol_ref, res_ref,
    live_ref, ids_ref, pix_ref, jac, proj, damp, prec, hot, direc, ufield,
    id_send, id_recv, back_send, back_recv, gath_send, gath_recv, sum_own, sum_recv,
    load_sem, ssem, rsem, issem, irsem,
):
    n_blk, n_pix, width = jac.shape
    n_proj, n_par, g_dev = proj.shape
    me = lax.axis_index("scene")
    img = lax.axis_index("image")
    device_pos = me * n_img + img

    small = [
        pltpu.make_async_copy(src, dst, load_sem.at[n_blk + 3 + i])
        for i, (src, dst) in enumerate(
            [(ids_hbm, ids_ref), (pix_hbm, pix_ref), (live_hbm, live_ref)]
        )
    ]
    for load in small:
        load.start()
    loads = [pltpu.make_async_copy(jac_hbm.at[b], jac.at[b], load_sem.at[b]) for b in range(n_blk)]
    loads.append(pltpu.make_async_copy(proj_hbm, proj, load_sem.at[n_blk]))
    loads.append(pltpu.make_async_copy(damp_hbm, damp, load_sem.at[n_blk + 1]))
    loads.append(pltpu.make_async_copy(prec_hbm, prec, load_sem.at[n_blk + 2]))
    for load in loads:
        load.start()

    scene_peers = [lax.rem(me + r, n) for r in range(1, n)]
    image_peers = [lax.rem(img + r, n_img) for r in range(1, n_img)]
    barrier = pltpu.get_barrier_semaphore()
    for peer in scene_peers:
        pl.semaphore_signal(barrier, inc=1, device_id={"scene": peer}, device_id_type=MESH)
    for peer in image_peers:
        pl.semaphore_signal(barrier, inc=1, device_id={"image": peer}, device_id_type=MESH)

    for load in small:
        load.wait()
    live = live_ref[device_pos]
    sends = []

    def remote(phase, send, recv, peer, r):
        return pltpu.make_async_remote_copy(
            src_ref=send.at[peer], dst_ref=recv.at[me],
            send_sem=ssem.at[phase, r], recv_sem=rsem.at[phase, me],
            device_id={"scene": peer}, device_id_type=MESH,
        )

    def exchange(phase, send, recv):
        for r, peer in enumerate(scene_peers):
            copy = remote(phase, send, recv, peer, r)
            copy.start()
            sends.append(copy)
        recv[me] = send[me]

    def wait_from(phase, recv, source):
        pltpu.make_async_remote_copy(
            src_ref=recv.at[source], dst_ref=recv.at[source],
            send_sem=ssem.at[phase, 0], recv_sem=rsem.at[phase, source],
            device_id={"scene": source}, device_id_type=MESH,
        ).wait_recv()

    def wait_all(phase, recv):
        for peer in scene_peers:
            wait_from(phase, recv, peer)

    n_pairs = n // 2
    pair_order = sorted(range(n_pairs), key=lambda o: min(o, n_pairs - o))
    pairs = [lax.rem(me // 2 + o, n_pairs) for o in pair_order]
    partner = me + 1 - 2 * lax.rem(me, 2)
    half = g_dev // 2

    def image_exchange(phase, h):
        copies = []
        for r, peer in enumerate(image_peers):
            copy = pltpu.make_async_remote_copy(
                src_ref=sum_own.at[phase, h], dst_ref=sum_recv.at[phase, h, img],
                send_sem=issem.at[phase, h, r], recv_sem=irsem.at[phase, h, r],
                device_id={"image": peer}, device_id_type=MESH,
            )
            copy.start()
            copies.append(copy)
        sum_recv[phase, h, img] = sum_own[phase, h]
        sends.extend(copies)
        return copies

    def pad_rows(x, fill):
        if n == n_blk:
            return x
        return jnp.concatenate([x, jnp.full((n - n_blk, LANES), fill, x.dtype)], axis=0)

    block_row = lax.broadcasted_iota(jnp.int32, (n_blk, width), 0)
    pix_row = lax.broadcasted_iota(jnp.int32, (n_blk, n_pix), 0)
    msg_row = lax.broadcasted_iota(jnp.int32, (ROWS, LANES), 0)

    def returned(signals, first):
        total = jnp.zeros((n_blk, width), F32)
        for b in range(n_blk):
            if first:
                loads[b].wait()
            one = jnp.dot(signals, jac[b], preferred_element_type=F32)
            total = jnp.where(block_row == b, one, total)
        return jnp.where(block_row < live, total, 0.0)

    def block_images(vectors):
        total = jnp.zeros((n_blk, n_pix), F32)
        for b in range(n_blk):
            total = jnp.where(pix_row == b, nt(vectors, jac[b]), total)
        return total.astype(BF16)

    def lane_sums(x):
        rows = jnp.sum(x, axis=0, keepdims=True)
        total = rows[:, :LANES]
        for c in range(1, x.shape[1] // LANES):
            total = total + rows[:, c * LANES:(c + 1) * LANES]
        return total

    def send_back(phase, back, extras):
        send, recv = back_send.at[phase], back_recv.at[phase]
        for k in range(n_proj):
            piece = pad_rows(back[:, k * LANES:(k + 1) * LANES], 0.0)
            send[:, k, :] = swap_groups(piece, n)
        for k in range(n_proj, ROWS):
            extra = extras[k - n_proj] if k - n_proj < len(extras) else jnp.zeros((1, LANES), F32)
            send[:, k, :] = jnp.broadcast_to(extra, (n, LANES))
        exchange(1 + 2 * phase, send, recv)

    def start_reduce(phase):
        recv = back_recv.at[phase]
        sums = [None, None]
        started = []
        for order, pair in enumerate(pairs):
            low = 2 * pair
            if order == 0:
                wait_from(1 + 2 * phase, recv, partner)
            else:
                wait_from(1 + 2 * phase, recv, low)
                wait_from(1 + 2 * phase, recv, low + 1)
            arrivals = jnp.concatenate([recv[low], recv[low + 1]], axis=1)
            parts = jnp.concatenate(split3(arrivals), axis=0)
            lanes = pl.ds(pl.multiple_of(pair * (2 * LANES), 2 * LANES), 2 * LANES)
            for h in range(2):
                one = nt(parts, hot[h * half:(h + 1) * half, lanes])
                sums[h] = one if order == 0 else sums[h] + one
        extras = recv[0]
        for j in range(1, n):
            extras = extras + recv[j]
        for h in range(2):
            summed = sums[h]
            summed = summed[:ROWS] + summed[ROWS:2 * ROWS] + summed[2 * ROWS:]
            sum_own[phase, h, :, :half] = summed[:8]
            sum_own[phase, h, :, half:] = jnp.where(
                msg_row[:8] == 7, extras[n_proj:n_proj + 1], 0.0
            )
            for c in range(half // LANES):
                sum_own[phase, h, c:c + 1, half:] = summed[8:9, c * LANES:(c + 1) * LANES]
            started.append(image_exchange(phase, h))
        side = jnp.sum(extras[n_proj + 1:n_proj + 2], keepdims=True)
        return started, side

    def finish_reduce(phase, h, copies):
        for copy in copies:
            copy.wait_recv()
        total = sum_recv[phase, h, 0]
        for i in range(1, n_img):
            total = total + sum_recv[phase, h, i]
        return total

    def lifted(weights, cols):
        here = cols.start % half
        chunk = here // LANES
        total = proj[8, :, cols].astype(F32) * weights[chunk:chunk + 1, half:]
        for k in range(8):
            total = total + proj[k, :, cols].astype(F32) * weights[k:k + 1, here:here + LANES]
        return total

    def chunks(h=None):
        first, last = (0, g_dev) if h is None else (h * half, (h + 1) * half)
        return [slice(c, c + LANES) for c in range(first, last, LANES)]

    def project_chunk(field, cols):
        for k in range(n_proj):
            ufield[k:k + 1, cols] = jnp.sum(
                proj[k, :, cols].astype(F32) * field, axis=0, keepdims=True
            )

    def send_gathered(phase, extras):
        parts = jnp.concatenate(split3(ufield[...]), axis=0)
        send, recv = gath_send.at[phase], gath_recv.at[phase]
        for order in reversed(range(n_pairs)):
            low = 2 * pairs[order]
            lanes = pl.ds(pl.multiple_of(pairs[order] * (2 * LANES), 2 * LANES), 2 * LANES)
            picked = jnp.dot(parts, hot[:, lanes], preferred_element_type=F32)
            picked = picked[:ROWS] + picked[ROWS:2 * ROWS] + picked[2 * ROWS:]
            for e in range(2):
                piece = picked[:, e * LANES:(e + 1) * LANES]
                for k, extra in enumerate(extras):
                    piece = jnp.where(msg_row == n_proj + k, extra, piece)
                send[low + e] = piece
            targets = [partner] if order == 0 else [low, low + 1]
            for e, target in enumerate(targets):
                r = 0 if order == 0 else 2 * order - 1 + e
                copy = remote(2 + 2 * phase, send, recv, target, r)
                copy.start()
                sends.append(copy)
        recv[me] = send[me]

    def take_gathered(phase):
        recv = gath_recv.at[phase]
        wait_all(2 + 2 * phase, recv)
        pieces = [swap_groups(recv[:, k, :], n)[:n_blk] for k in range(n_proj)]
        extras = recv[0]
        for j in range(1, n):
            extras = extras + recv[j]
        sums = jnp.sum(extras, axis=1, keepdims=True)
        return jnp.concatenate(pieces, axis=1), sums[n_proj:n_proj + 1], sums[n_proj + 1:n_proj + 2]

    routed = swap_groups(pad_rows(ids_ref[...], -1), n)
    id_send[:, 0, :] = routed
    pl.semaphore_wait(barrier, n - 1 + n_img - 1)
    exchange(0, id_send, id_recv)

    back = returned(pix_ref[...], True)
    send_back(0, back, [])

    wait_all(0, id_recv)
    ufield[...] = jnp.zeros_like(ufield)
    g_iota = lax.broadcasted_iota(jnp.int32, (g_dev, LANES), 0)
    for j in range(n):
        local_ids = id_recv[j] - me * g_dev
        hot[:, j * LANES:(j + 1) * LANES] = jnp.where(g_iota == local_ids, 1.0, 0.0).astype(BF16)
    for load in loads[n_blk:]:
        load.wait()

    started, _ = start_reduce(0)
    rz_part = jnp.zeros((1, LANES), F32)
    dd_part = jnp.zeros((1, LANES), F32)
    for h in range(2):
        weights = finish_reduce(0, h, started[h])
        for cols in chunks(h):
            residual = -lifted(weights, cols)
            res_ref[:, cols] = residual
            z = prec[:, cols] * residual
            direc[:, cols] = z
            rz_part = rz_part + jnp.sum(residual * z, axis=0, keepdims=True)
            dd_part = dd_part + jnp.sum(damp[:, cols] * z * z, axis=0, keepdims=True)
            project_chunk(z, cols)
    send_gathered(0, [rz_part, dd_part])

    vectors = rz_now = None
    for iteration in range(ITERS):
        if iteration == 0:
            vectors, rz_now, dd = take_gathered(0)
        else:
            gathered, rz_next, _ = take_gathered(iteration)
            beta = rz_next / rz_now
            rz_now = rz_next
            vectors = gathered + beta * vectors
        back = returned(block_images(vectors.astype(BF16)), False)
        extras = []
        if iteration > 0:
            dd_part = jnp.zeros((1, LANES), F32)
            for cols in chunks():
                d = prec[:, cols] * res_ref[:, cols] + beta * direc[:, cols]
                direc[:, cols] = d
                dd_part = dd_part + jnp.sum(damp[:, cols] * d * d, axis=0, keepdims=True)
            extras = [dd_part]
        send_back(iteration + 1, back, [lane_sums(back * vectors)] + extras)
        started, side = start_reduce(iteration + 1)
        last = iteration == ITERS - 1
        rz_part = jnp.zeros((1, LANES), F32)
        for h in range(2):
            weights = finish_reduce(iteration + 1, h, started[h])
            if h == 0:
                dot = jnp.sum(weights[7:8, half:], keepdims=True)
                alpha = rz_now / (dot + (dd if iteration == 0 else side))
            for cols in chunks(h):
                d = direc[:, cols]
                image = lifted(weights, cols) + damp[:, cols] * d
                residual = res_ref[:, cols] - alpha * image
                res_ref[:, cols] = residual
                sol_ref[:, cols] = alpha * d if iteration == 0 else sol_ref[:, cols] + alpha * d
                if not last:
                    z = prec[:, cols] * residual
                    rz_part = rz_part + jnp.sum(residual * z, axis=0, keepdims=True)
                    project_chunk(z, cols)
        if not last:
            send_gathered(iteration + 1, [rz_part])
    for copy in sends:
        copy.wait_send()


def local(n, n_img, jacobian, splat_ids, pix_residual, live_blocks, proj_jac, damping, precond):
    n_blk, n_pix, width = jacobian.shape
    n_proj, n_par, g_dev = proj_jac.shape
    field = (n_par, g_dev)
    phases = 2 * ITERS + 2
    vmem = pl.BlockSpec(memory_space=pltpu.VMEM)
    hbm = pl.BlockSpec(memory_space=pltpu.HBM)
    return pl.pallas_call(
        functools.partial(kernel, n, n_img),
        out_shape=[jax.ShapeDtypeStruct(field, F32)] * 2,
        in_specs=[hbm] * 7,
        out_specs=[vmem, vmem],
        scratch_shapes=[
            pltpu.SMEM(live_blocks.shape, jnp.int32),
            pltpu.VMEM(splat_ids.shape, jnp.int32),
            pltpu.VMEM(pix_residual.shape, BF16),
            pltpu.VMEM(jacobian.shape, BF16),
            pltpu.VMEM(proj_jac.shape, BF16),
            pltpu.VMEM(field, F32),
            pltpu.VMEM(field, F32),
            pltpu.VMEM((g_dev, n * LANES), BF16),
            pltpu.VMEM(field, F32),
            pltpu.VMEM((ROWS, g_dev), F32),
            pltpu.VMEM((n, 1, LANES), jnp.int32),
            pltpu.VMEM((n, 1, LANES), jnp.int32),
            pltpu.VMEM((ITERS + 1, n, ROWS, LANES), F32),
            pltpu.VMEM((ITERS + 1, n, ROWS, LANES), F32),
            pltpu.VMEM((ITERS, n, ROWS, LANES), F32),
            pltpu.VMEM((ITERS, n, ROWS, LANES), F32),
            pltpu.VMEM((ITERS + 1, 2, 8, g_dev // 2 + LANES), F32),
            pltpu.VMEM((ITERS + 1, 2, n_img, 8, g_dev // 2 + LANES), F32),
            pltpu.SemaphoreType.DMA((n_blk + 6,)),
            pltpu.SemaphoreType.DMA((phases, n - 1)),
            pltpu.SemaphoreType.DMA((phases, n)),
            pltpu.SemaphoreType.DMA((ITERS + 1, 2, n_img - 1)),
            pltpu.SemaphoreType.DMA((ITERS + 1, 2, n_img - 1)),
        ],
        compiler_params=pltpu.CompilerParams(
            collective_id=0, has_side_effects=True, vmem_limit_bytes=67043328
        ),
    )(live_blocks, splat_ids, pix_residual, jacobian, proj_jac, damping, precond)


def solution(mesh):
    return jax.shard_map(
        functools.partial(local, mesh.shape["scene"], mesh.shape["image"]),
        mesh=mesh,
        in_specs=(
            P(("scene", "image"), None, None),
            P(("scene", "image"), None),
            P(("scene", "image"), None),
            P(),
            P(None, None, "scene"),
            P(None, "scene"),
            P(None, "scene"),
        ),
        out_specs=(P(None, "scene"), P(None, "scene")),
        check_vma=False,
    )
```
